128 devices in a mesh: tm: 32 (over y, z, core), mel: 4 (over x).
Axes of the slice: x: 4, y: 4, z: 4, core: 2. Of those that a mesh axis runs over, the one named last changes fastest.
Arguments:
- act_one: bfloat16 [4096, 16384], P('tm', 'mel'), may hold values from -6 to 6
- act_two: bfloat16 [4096, 16384], P('tm', 'mel'), may hold values from -6 to 6
- act_three: bfloat16 [2048, 16384], P('tm', 'mel'), may hold values from -6 to 6
- act_four: bfloat16 [2048, 16384], P('tm', 'mel'), may hold values from -6 to 6
- target_one: bfloat16 [2048, 8192], P('tm', 'mel'), may hold values from -6 to 6
- target_two: bfloat16 [1024, 8192], P('tm', 'mel'), may hold values from -6 to 6
- kernel_one: bfloat16 [3, 3, 1, 64], replicated, may hold values from -2 to 2
- kernel_two: bfloat16 [3, 3, 64, 64], replicated, may hold values from -0.25 to 0.25
- kernel_three: bfloat16 [3, 3, 64, 128], replicated, may hold values from -0.25 to 0.25
- kernel_four: bfloat16 [3, 3, 128, 128], replicated, may hold values from -0.1875 to 0.1875
- mel_power: float32 [4096, 256], P('tm', 'mel'), may hold values from 0.05 to 20
- loudness: float32 [256], P('mel'), may hold values from 0.1 to 10
- filters: float32 [512, 256], replicated, may hold values from -0.375 to 0.375
- spec_real: float32 [4096, 512], P('tm', 'mel'), may hold values from -6 to 6
- spec_imag: float32 [4096, 512], P('tm', 'mel'), may hold values from -6 to 6
Outputs:
- wave_grad: float32 [2097152], P(('tm', 'mel'))
The draws below stay inside these ranges and needn't reach their ends.
All inputs are finite; a program needn't handle non-finite values.
Results may differ from the reference program's by a relative error of at most 0.015.
Values may be sent and summed in bfloat16 or wider, within the bound.
No kernel may reach another device: no remote copies, remote signals or barrier semaphores. Data moves between devices by JAX's collectives and lax.ppermute only.
A program may use at most 64 MiB of HBM per device.

```python
import math
import jax
import jax.numpy as jnp
from jax import lax

MELS = 256
C1 = 64
C2 = 128
NFFT = 1024
BINS = 512
HOP = 512
FRAMES = 4096
SAMPLES = 2097152


def steps_of(stream_key, dims, pieces, low, top_value):
    def one(axis_at, shards_of):
        steps = jax.random.uniform(jax.random.fold_in(jax.random.fold_in(stream_key, 6), axis_at), (shards_of,), jnp.float32, low / len(pieces), top_value / len(pieces))
        return jnp.repeat(jnp.exp(steps), dims[axis_at] // shards_of).reshape((-1,) + (1,) * (len(dims) - axis_at - 1))

    level = one(*pieces[0])
    for cut in pieces[1:]:
        level = level * one(*cut)
    return level


def noise(key, shape, deviation, reach, cuts=(), kind=jnp.bfloat16):
    level = steps_of(key, shape, cuts, -0.22, 0.18) if cuts else 1.0
    values = jax.random.normal(key, shape, jnp.float32) * deviation * level
    return jnp.minimum(jnp.maximum(values, -reach), reach).astype(kind)


def setup_inputs(seed: int = 0) -> dict:
    key_of = jax.random.split(jax.random.key(seed), 16)
    return {
        "act_one": noise(key_of[0], (FRAMES, MELS * C1), 1.0, 6.0, ((0, 32), (1, 4))),
        "act_two": noise(key_of[1], (FRAMES, MELS * C1), 1.0, 6.0, ((0, 32), (1, 4))),
        "act_three": noise(key_of[2], (FRAMES // 2, MELS // 2 * C2), 1.0, 6.0, ((0, 32), (1, 4))),
        "act_four": noise(key_of[3], (FRAMES // 2, MELS // 2 * C2), 1.0, 6.0, ((0, 32), (1, 4))),
        "target_one": noise(key_of[4], (FRAMES // 2, MELS // 2 * C1), 1.0, 6.0, ((0, 32), (1, 4))),
        "target_two": noise(key_of[5], (FRAMES // 4, MELS // 4 * C2), 1.0, 6.0, ((0, 32), (1, 4))),
        "kernel_one": noise(key_of[6], (3, 3, 1, C1), 9 ** -0.5, 2.0),
        "kernel_two": noise(key_of[7], (3, 3, C1, C1), (9 * C1) ** -0.5, 0.25),
        "kernel_three": noise(key_of[8], (3, 3, C1, C2), (9 * C1) ** -0.5, 0.25),
        "kernel_four": noise(key_of[9], (3, 3, C2, C2), (9 * C2) ** -0.5, 0.1875),
        "mel_power": jnp.clip(jnp.exp(math.log(20.0) - 5.9914645 * jax.random.uniform(key_of[10], (FRAMES, MELS), jnp.float32) ** steps_of(key_of[10], (FRAMES, MELS), ((0, 32), (1, 4)), -0.2, 0.2)), 0.05, 20.0),
        "loudness": jnp.clip(jnp.exp(math.log(10.0) - 4.6051702 * jax.random.uniform(key_of[11], (MELS,), jnp.float32) ** steps_of(key_of[11], (MELS,), ((0, 4),), -0.2, 0.2)), 0.1, 10.0),
        "filters": noise(key_of[12], (BINS, MELS), MELS ** -0.5, 0.375, (), jnp.float32),
        "spec_real": noise(key_of[13], (FRAMES, BINS), 1.0, 6.0, ((0, 32), (1, 4)), jnp.float32),
        "spec_imag": noise(key_of[14], (FRAMES, BINS), 1.0, 6.0, ((0, 32), (1, 4)), jnp.float32),
    }


def pool(values):
    rows, cols, chans = values.shape
    return 0.25 * jnp.sum(values.reshape(rows // 2, 2, cols // 2, 2, chans), axis=(1, 3))


def spread(grad):
    rows, cols, chans = grad.shape
    wide = jnp.broadcast_to(grad[:, None, :, None, :], (rows, 2, cols, 2, chans))
    return 0.25 * wide.reshape(rows * 2, cols * 2, chans)


def back_conv(grad, weights):
    kernel = jnp.transpose(weights[::-1, ::-1], (0, 1, 3, 2)).astype(jnp.float32)
    return lax.conv_general_dilated(grad.astype(jnp.float32)[None], kernel, (1, 1), ((1, 1), (1, 1)), dimension_numbers=("NHWC", "HWIO", "NHWC"), precision=lax.Precision.HIGHEST)[0]


def dft_table(offset, count):
    freqs = offset + jnp.arange(count, dtype=jnp.int32)
    points = jnp.arange(NFFT, dtype=jnp.int32)
    phase = (freqs[:, None] * points[None, :]) % NFFT
    angle = phase.astype(jnp.float32) * (2.0 * jnp.pi / NFFT)
    return jnp.concatenate([jnp.cos(angle), -jnp.sin(angle)], axis=0)


def reference(act_one, act_two, act_three, act_four, target_one, target_two, kernel_one, kernel_two, kernel_three, kernel_four, mel_power, loudness, filters, spec_real, spec_imag):
    first = act_one.reshape(FRAMES, MELS, C1)
    second = act_two.reshape(FRAMES, MELS, C1)
    third = act_three.reshape(FRAMES // 2, MELS // 2, C2)
    fourth = act_four.reshape(FRAMES // 2, MELS // 2, C2)
    feat_low = pool(jnp.maximum(second.astype(jnp.float32), 0.0))
    feat_high = pool(jnp.maximum(fourth.astype(jnp.float32), 0.0))
    diff_high = feat_high - target_two.reshape(FRAMES // 4, MELS // 4, C2).astype(jnp.float32)
    grad_four = jnp.where(fourth > 0, spread(diff_high), 0.0).astype(jnp.bfloat16)
    grad_three = jnp.where(third > 0, back_conv(grad_four, kernel_four), 0.0).astype(jnp.bfloat16)
    grad_pool = back_conv(grad_three, kernel_three) + feat_low - target_one.reshape(FRAMES // 2, MELS // 2, C1).astype(jnp.float32)
    grad_two = jnp.where(second > 0, spread(grad_pool), 0.0).astype(jnp.bfloat16)
    grad_one = jnp.where(first > 0, back_conv(grad_two, kernel_two), 0.0).astype(jnp.bfloat16)
    grad_log = back_conv(grad_one, kernel_one)[:, :, 0]
    grad_mel = grad_log * loudness[None, :] / (1.0 + loudness[None, :] * mel_power)
    grad_power = lax.dot_general(grad_mel, filters, (((1,), (1,)), ((), ())), precision=lax.Precision.HIGHEST)
    grad_re = 2.0 * grad_power * spec_real
    grad_im = 2.0 * grad_power * spec_imag
    points = jnp.arange(NFFT, dtype=jnp.int32).astype(jnp.float32)
    window = 0.5 - 0.5 * jnp.cos(points * (2.0 * jnp.pi / NFFT))
    frames = jnp.dot(jnp.concatenate([grad_re, grad_im], axis=1), dft_table(0, BINS), precision=lax.Precision.HIGHEST)
    frames = frames * window[None, :] * (NFFT ** -0.5)
    shifted = jnp.concatenate([jnp.zeros((1, HOP), jnp.float32), frames[:-1, HOP:]], axis=0)
    return (frames[:, :HOP] + shifted).reshape(SAMPLES)
```

```python
import numpy as np
import jax
import jax.numpy as jnp
from jax import lax
from jax.experimental import pallas as pl
from jax.experimental.pallas import tpu as pltpu
from jax.sharding import PartitionSpec as P

F32 = jnp.float32
BF16 = jnp.bfloat16
C1 = 64
C2 = 128
NFFT = 1024
HOP = 512
L = 128
RC = 80
RF = 144
VMEM = pl.BlockSpec(memory_space=pltpu.VMEM)
SMEM = pl.BlockSpec(memory_space=pltpu.SMEM)
ROWS_M = 784


def lanes(index, width=L):
    return pl.ds(index * width, width)


def dot(lhs, rhs):
    return jnp.dot(lhs, rhs, preferred_element_type=F32)


def swap_halves(value):
    return pltpu.roll(value, 64, axis=1)


def lower_lanes(shape):
    return lax.broadcasted_iota(jnp.int32, shape, 1) < 64


def call(kernel, outs, scratch, args, specs=None, limit=24, flops=0, moved=1 << 20):
    return pl.pallas_call(
        kernel,
        out_shape=[jax.ShapeDtypeStruct(s, d) for s, d in outs],
        in_specs=specs or [VMEM] * len(args),
        out_specs=[VMEM] * len(outs),
        scratch_shapes=[pltpu.VMEM(s, d) for s, d in scratch],
        compiler_params=pltpu.CompilerParams(vmem_limit_bytes=limit << 20),
        cost_estimate=pl.CostEstimate(flops=flops, bytes_accessed=moved, transcendentals=0),
    )(*args)


def pack_rows_kernel(
    four_end, four_top, three_end, three_top, two_end, two_top, one_end, one_top,
    high_end, high_top, low_end, low_top, mel_end, re_end, im_end,
    end_out, top_out, tmp, end, top,
):
    end[...] = jnp.zeros_like(end)
    top[...] = jnp.zeros_like(top)
    for source, dest, first, count, row in (
        (four_end, end, 12, 4, 0),
        (three_end, end, 13, 3, 4),
        (two_end, end, 12, 4, 7),
        (one_end, end, 14, 2, 11),
        (four_top, top, 0, 4, 0),
        (three_top, top, 0, 2, 4),
        (two_top, top, 0, 2, 6),
        (one_top, top, 0, 1, 8),
    ):
        tmp[...] = source[...].astype(F32)
        dest[row : row + count, :] = tmp[first : first + count, :]
    for source, dest, first, count, row in (
        (high_end, end, 14, 2, 13),
        (low_end, end, 14, 2, 14),
        (high_top, top, 0, 2, 9),
        (low_top, top, 0, 1, 10),
    ):
        tmp[:, 0:2048] = source[...].astype(F32)
        for k in range(count):
            dest[row : row + 1, k * 2048 : (k + 1) * 2048] = tmp[first + k : first + k + 1, 0:2048]
    tmp[0:8, 0:64] = mel_end[...]
    mel = tmp[7:8, 0:64]
    head = mel.astype(BF16).astype(F32)
    end[15:16, 0:64] = head
    end[15:16, 128:192] = mel - head
    tmp[0:8, 256:384] = re_end[...]
    tmp[0:8, 384:512] = im_end[...]
    end[15:16, 256:512] = tmp[7:8, 256:512]
    end_out[...] = end[...].astype(BF16)
    top_out[...] = top[...].astype(BF16)


def pack_rows(a4, a3, a2, a1, t2, t1, mel, re, im):
    ends = {64: 3, 128: 7, 32: 1}
    args, specs = [], []
    for value in (a4, a3, a2, a1, t2, t1):
        rows, cols = value.shape
        for block in (ends[rows], 0):
            args.append(value)
            specs.append(pl.BlockSpec((16, cols), lambda i, block=block: (block, 0)))
    for value in (mel, re, im):
        args.append(value)
        specs.append(pl.BlockSpec((8, value.shape[1]), lambda i: (15, 0)))
    return pl.pallas_call(
        pack_rows_kernel,
        out_shape=[jax.ShapeDtypeStruct((16, 4096), BF16)] * 2,
        grid=(1,),
        in_specs=specs,
        out_specs=[VMEM] * 2,
        scratch_shapes=[pltpu.VMEM((16, 4096), F32)] * 3,
        compiler_params=pltpu.CompilerParams(vmem_limit_bytes=16 << 20),
    )(*args)


def halo_tiles(before, after, raw, tiles, tiles_two, tiles_one, span):
    raw[0, :, span] = before[:, span].astype(F32)
    raw[1, :, span] = after[:, span].astype(F32)
    for k, (dest, first, count, side) in enumerate(
        (
            (4, 0, 4, 0),
            (5, 4, 3, 0),
            (4, 7, 4, 0),
            (6, 11, 2, 0),
            (0, 0, 4, 1),
            (0, 4, 2, 1),
            (0, 6, 2, 1),
            (0, 8, 1, 1),
        )
    ):
        tiles[k, :, span] = jnp.zeros_like(tiles[k, :, span])
        tiles[k, dest : dest + count, span] = raw[side, first : first + count, span]


def target_tiles(before, after, raw, tiles_two, tiles_one):
    raw[0] = before[...].astype(F32)
    raw[1] = after[...].astype(F32)
    tiles_two[...] = jnp.zeros_like(tiles_two)
    tiles_one[...] = jnp.zeros_like(tiles_one)
    for k in range(2):
        half = slice(k * 2048, (k + 1) * 2048)
        tiles_two[0, 6 + k : 7 + k, :] = raw[0, 13:14, half]
        tiles_two[1, k : k + 1, :] = raw[1, 9:10, half]
        tiles_one[0, 6 + k : 7 + k, :] = raw[0, 14:15, half]
    tiles_one[1, 0:1, :] = raw[1, 10:11, 0:2048]


def padded(ref, tiles, kind, span):
    return jnp.concatenate(
        [tiles[kind, :, span], ref[:, span].astype(F32), tiles[kind + 4, :, span]], axis=0
    )


def repeat_rows_matrix():
    r = lax.broadcasted_iota(jnp.int32, (RC, 48), 0)
    x = lax.broadcasted_iota(jnp.int32, (RC, 48), 1)
    return jnp.where(x == lax.shift_right_logical(r, 1) + 4, 1.0, 0.0).astype(BF16)


def repeated_target(ref, tiles, span):
    values = jnp.concatenate([tiles[0, :, span], ref[:, span].astype(F32), tiles[1, :, span]], axis=0)
    return dot(repeat_rows_matrix(), values.astype(BF16))


def pooled_grads(first, second, target):
    both = jnp.maximum(first, 0.0) + jnp.maximum(second, 0.0)
    cells = both.reshape(RC // 8, 8, L)
    even = lax.broadcasted_iota(jnp.int32, cells.shape, 1) % 2 == 0
    other = jnp.where(even, pltpu.roll(cells, 7, axis=1), pltpu.roll(cells, 1, axis=1))
    feat = 0.25 * (cells + other).reshape(RC, L)
    diff = 0.25 * (feat - target)
    return jnp.where(first > 0, diff, 0.0), jnp.where(second > 0, diff, 0.0)


def lane_doubled(value, upper):
    swapped = swap_halves(value)
    low = lower_lanes(value.shape)
    return jnp.where(low, swapped, value) if upper else jnp.where(low, value, swapped)


def pack_columns_kernel(
    place, a4, a3, a2, a1, t2, t1, re, im, before, after,
    left_out, right_out, far_out, own_out, raw, tiles, tiles_two, tiles_one, spec, blocks,
):
    target_tiles(before, after, raw, tiles_two, tiles_one)
    for span in (slice(0, 512), slice(3584, 4096)):
        halo_tiles(before, after, raw, tiles, tiles_two, tiles_one, span)
    mel = place[0]
    spec[...] = jnp.zeros_like(spec)
    spec[8:136, 0:128] = re[...]
    spec[8:136, 128:256] = im[...]
    spec[7:8, :] = raw[0, 15:16, 256:512]
    for d in range(4):
        part = spec[7 + 32 * d : 55 + 32 * d, :]
        blocks[d, 0:48, :] = part[:, 0:128].astype(BF16)
        blocks[d, 48:96, :] = part[:, 128:256].astype(BF16)
    own_out[...] = blocks[mel]
    far_out[...] = blocks[lax.rem(mel + 2, 4)]
    left_out[688:784, :] = blocks[lax.rem(mel + 3, 4)]
    right_out[688:784, :] = blocks[lax.rem(mel + 1, 4)]
    keep_left = jnp.where(mel > 0, 1.0, 0.0).astype(F32)
    keep_right = jnp.where(mel < 3, 1.0, 0.0).astype(F32)
    for out, keep, pairs, wanted, three, edge, upper in (
        (left_out, keep_left, (0, 1), (0, 1, 2), (0, 1), 0, False),
        (right_out, keep_right, (14, 15), (29, 30, 31), (30, 31), 31, True),
    ):
        for p in pairs:
            columns = [padded(a4, tiles, 0, lanes(2 * p + k)) for k in range(2)]
            target = repeated_target(t2, tiles_two, lanes(p))
            for k, grad in enumerate(pooled_grads(*columns, target)):
                if 2 * p + k in wanted:
                    at = wanted.index(2 * p + k) * RC
                    out[at : at + RC, :] = (grad * keep).astype(BF16)
        for k, c in enumerate(three):
            at = 240 + k * RC
            out[at : at + RC, :] = (padded(a3, tiles, 1, lanes(c)) * keep).astype(BF16)
        out[400:544, :] = (padded(a2, tiles, 2, lanes(edge)) * keep).astype(BF16)
        one = padded(a1, tiles, 3, lanes(edge))
        low_target = jnp.concatenate(
            [
                tiles_one[0, :, lanes(edge // 2)],
                t1[:, lanes(edge // 2)].astype(F32),
                tiles_one[1, :, lanes(edge // 2)],
            ],
            axis=0,
        )
        low_target = jnp.concatenate([low_target, jnp.zeros((RF - RC, L), F32)], axis=0)
        swapped = swap_halves(low_target)
        low = lower_lanes((RF, L))
        joined = jnp.where(low, swapped, one) if upper else jnp.where(low, one, swapped)
        out[544:688, :] = (joined * keep).astype(BF16)


def weights_kernel(k4, k3, k2, k1, w4, w3, w2, w1):
    w4[...] = jnp.zeros_like(w4)
    w3[...] = jnp.zeros_like(w3)
    w2[...] = jnp.zeros_like(w2)
    for i in range(3):
        for b in range(4):
            row = (i * 4 + b) * L
            for a in range(2):
                j = 1 + a - b
                if -1 <= j <= 1:
                    w4[row : row + L, a * L : (a + 1) * L] = k4[i, j + 1]
            w3[row : row + L, :] = jnp.concatenate(
                [k3[i, 2 + a - b] if -1 <= 1 + a - b <= 1 else jnp.zeros((L, L), BF16) for a in range(2)], axis=1
            )
            row = (i * 4 + b) * 64
            parts = [k2[i, 2 + a - b] if -1 <= 1 + a - b <= 1 else jnp.zeros((64, L), BF16) for a in range(2)]
            w2[row : row + 64, :] = jnp.where(lower_lanes((64, L)), parts[0], parts[1])
    shape = (L, 256)
    lane = lax.broadcasted_iota(jnp.int32, shape, 1)
    parity = lax.shift_right_logical(lax.broadcasted_iota(jnp.int32, shape, 0), 6)
    column = lane - parity
    spot = lax.bitwise_and(lane, 63)

    def direct(p):
        total = jnp.zeros(shape, F32)
        for i in range(3):
            for j in (-1, 0, 1):
                hit = column == i * 64 + 2 * p + j
                fits = (2 * p + parity + j >= 0) & (2 * p + parity + j < 64)
                weight = jnp.broadcast_to(k1[:, i * 3 + j + 1 : i * 3 + j + 2], shape)
                total = jnp.where(hit & fits, weight, total)
        return total

    base = direct(1)
    for p in range(-1, 33):
        value = direct(p) if p in (-1, 0, 31, 32) else base if p == 1 else pltpu.roll(base, 2 * (p - 1), axis=1)
        w1[(p + 1) * L : (p + 2) * L, :] = value.astype(BF16)


def write_shifted(value, rows, pad, stores):
    pad[8 : 8 + rows, :] = value
    for i, store in enumerate(stores):
        store(pad[9 - i : 9 - i + rows, :].astype(BF16))


def pool_rows_matrix():
    r = lax.broadcasted_iota(jnp.int32, (RC, RF), 0)
    x = lax.broadcasted_iota(jnp.int32, (RC, RF), 1)
    return jnp.where(lax.shift_right_logical(x, 1) + 4 == r, 1.0, 0.0).astype(BF16)


def spread_rows_matrix():
    x = lax.broadcasted_iota(jnp.int32, (RF, RC), 0)
    r = lax.broadcasted_iota(jnp.int32, (RF, RC), 1)
    return jnp.where(lax.shift_right_logical(x, 1) + 4 == r, 1.0, 0.0).astype(BF16)


def pooled_low(second):
    rows = dot(pool_rows_matrix(), jnp.maximum(second, 0.0).astype(BF16))
    return 0.25 * (rows + swap_halves(rows))


def joined(parts):
    return jnp.concatenate(parts, axis=-1)


def interior_kernel(
    a4, a3, a2, a1, t2, t1, before, after, mel, loud, w4, w3, w2, w1,
    edge_g4, edge_g3, edge_g2, edge_a3, edge_a2, edge_low, edge_a1, part_out, factor_out,
    raw, tiles, tiles_two, tiles_one, even4, odd4, even3, odd3, back2, grad1, pad_c, pad_f, t2s,
):
    target_tiles(before, after, raw, tiles_two, tiles_one)
    halo_tiles(before, after, raw, tiles, tiles_two, tiles_one, slice(0, 4096))
    pad_c[...] = jnp.zeros_like(pad_c)
    pad_f[...] = jnp.zeros_like(pad_f)
    pad_f[8:136, 0:64] = mel[...]
    pad_f[7:8, 0:64] = raw[0, 15:16, 0:64] + raw[0, 15:16, 128:192]
    gain = loud[0:1, :]
    factor_out[...] = jnp.zeros_like(factor_out)
    factor_out[:, 0:64] = gain / (1.0 + gain * pad_f[0:RF, 0:64])
    t2s[...] = repeated_target(t2, tiles_two, slice(0, 2048))

    for p in range(16):
        columns = [padded(a4, tiles, 0, lanes(2 * p + k)) for k in range(2)]
        grads = pooled_grads(*columns, t2s[:, lanes(p)])
        if p in (0, 15):
            for k in range(2):
                edge_g4[(0 if p == 0 else 2) + k] = grads[k].astype(BF16)
        for k, store in enumerate((even4, odd4)):
            write_shifted(grads[k], RC, pad_c, [lambda v, i=i: store.__setitem__((i, p), v) for i in range(3)])
    lhs = joined([x for i in range(3) for x in (even4[i, 0:15], odd4[i, 0:15], even4[i, 1:16], odd4[i, 1:16])])
    out = dot(lhs.reshape(15 * RC, 1536), w4[...]).reshape(15, RC, 256)
    for q in range(15):
        for k, store in enumerate((odd3, even3)):
            c = 2 * q + 1 + k
            grad = jnp.where(padded(a3, tiles, 1, lanes(c)) > 0, out[q, :, k * L : (k + 1) * L], 0.0)
            if c in (1, 2, 29, 30):
                edge_g3[(1, 2, 29, 30).index(c)] = grad.astype(BF16)
            write_shifted(grad, RC, pad_c, [lambda v, i=i: store.__setitem__((i, q), v) for i in range(3)])
    for k, c in enumerate((0, 31)):
        edge_a3[k] = padded(a3, tiles, 1, lanes(c)).astype(BF16)
    lhs = joined([x for i in range(3) for x in (odd3[i, 0:14], even3[i, 0:14], odd3[i, 1:15], even3[i, 1:15])])
    out = dot(lhs.reshape(14 * RC, 1536), w3[...]).reshape(14, RC, 256)

    def low_loss(c, second):
        span = lanes(c // 2)
        target = jnp.concatenate([tiles_one[0, :, span], t1[:, span].astype(F32), tiles_one[1, :, span]], axis=0)
        return pooled_low(second) - lane_doubled(target, c % 2 == 1)

    for k, c in enumerate((0, 1, 30, 31)):
        second = padded(a2, tiles, 2, lanes(c))
        edge_a2[k] = second.astype(BF16)
        edge_low[k] = low_loss(c, second)
    spreading = spread_rows_matrix()
    last = None
    for c in range(2, 30):
        second = padded(a2, tiles, 2, lanes(c))
        grad = out[c // 2 - 1, :, (c % 2) * L : (c % 2 + 1) * L] + low_loss(c, second)
        wide = dot(spreading, (0.25 * grad).astype(BF16))
        fine = jnp.where(second > 0, wide, 0.0)
        if c in (2, 3, 28, 29):
            edge_g2[(2, 3, 28, 29).index(c)] = fine.astype(BF16)
        turned = swap_halves(fine)
        if last is not None:
            window = jnp.where(lower_lanes((RF, L)), last, turned)
            write_shifted(window, RF, pad_f, [lambda v, i=i: back2.__setitem__((i, c - 3), v) for i in range(3)])
        last = turned
    lhs = joined([x for i in range(3) for x in (back2[i, 0:26], back2[i, 1:27])])
    out = dot(lhs.reshape(26 * RF, 768), w2[...]).reshape(26, RF, L)
    for p in range(3, 29):
        grad = jnp.where(padded(a1, tiles, 3, lanes(p)) > 0, out[p - 3], 0.0)
        grad1[:, lanes(p - 3)] = grad.astype(BF16)
    for k, p in enumerate((0, 1, 2, 29, 30, 31)):
        edge_a1[k] = padded(a1, tiles, 3, lanes(p)).astype(BF16)
    part_out[...] = dot(grad1[...], w1[4 * L : 30 * L, :])


def edge_kernel(
    from_left, from_right, edge_g4, edge_g3, edge_g2, edge_a3, edge_a2, edge_low, edge_a1,
    part, factor, w4, w3, w2, w1, out_ref, shift4, shift3, back2, grad1, pad_c, pad_f, sums,
):
    pad_c[...] = jnp.zeros_like(pad_c)
    pad_f[...] = jnp.zeros_like(pad_f)
    zero_c = jnp.zeros((RC, L), F32)
    zero_f = jnp.zeros((RF, L), F32)

    def block(ref, at, rows):
        return ref[at : at + rows, :].astype(F32)

    def put(store, index, value, rows, pad):
        write_shifted(value, rows, pad, [lambda v, i=i: store.__setitem__((i, index), v) for i in range(3)])

    left, right = from_left, from_right
    columns = [zero_c] + [block(left, k * RC, RC) for k in range(3)] + [edge_g4[k].astype(F32) for k in range(4)]
    columns += [block(right, k * RC, RC) for k in range(3)] + [zero_c]
    for k, value in enumerate(columns):
        put(shift4, k, value, RC, pad_c)
    starts = (0, 2, 6, 8)
    lhs = jnp.concatenate(
        [joined([shift4[i, s + b] for i in range(3) for b in range(4)]) for s in starts], axis=0
    )
    out = dot(lhs, w4[...])
    masks = [zero_c, block(left, 240, RC), block(left, 240 + RC, RC), edge_a3[0].astype(F32)]
    masks += [edge_a3[1].astype(F32), block(right, 240, RC), block(right, 240 + RC, RC), zero_c]
    threes = []
    for k in range(8):
        value = out[(k // 2) * RC : (k // 2 + 1) * RC, (k % 2) * L : (k % 2 + 1) * L]
        threes.append(jnp.where(masks[k] > 0, value, 0.0))
    columns = threes[0:4] + [edge_g3[k].astype(F32) for k in range(4)] + threes[4:8]
    for k, value in enumerate(columns):
        put(shift3, k, value, RC, pad_c)
    lhs = jnp.concatenate(
        [joined([shift3[i, s + b] for i in range(3) for b in range(4)]) for s in starts], axis=0
    )
    out = dot(lhs, w3[...])
    spreading = spread_rows_matrix()
    twos = []
    for k in (1, 2, 3, 4, 5, 6):
        grad = out[(k // 2) * RC : (k // 2 + 1) * RC, (k % 2) * L : (k % 2 + 1) * L]
        if k in (1, 6):
            ref = left if k == 1 else right
            second = block(ref, 400, RF)
            target = block(ref, 544, RC)
            low = pooled_low(second) - lane_doubled(target, k == 6)
        else:
            second = edge_a2[k - 2].astype(F32)
            low = edge_low[k - 2]
        wide = dot(spreading, (0.25 * (grad + low)).astype(BF16))
        twos.append(jnp.where(second > 0, wide, 0.0))
    turned = [swap_halves(x) for x in twos]
    inner = [swap_halves(edge_g2[k].astype(F32)) for k in range(4)]
    low = lower_lanes((RF, L))
    chain = [zero_f] + turned[0:3] + inner[0:2]
    windows = [jnp.where(low, chain[k], chain[k + 1]) for k in range(5)]
    chain = inner[2:4] + turned[3:6] + [zero_f]
    windows += [jnp.where(low, chain[k], chain[k + 1]) for k in range(5)]
    for k, value in enumerate(windows):
        put(back2, k, value, RF, pad_f)
    lhs = jnp.concatenate(
        [joined([back2[i, s + b] for i in range(3) for b in range(2)]) for s in (0, 1, 2, 3, 5, 6, 7, 8)], axis=0
    )
    out = dot(lhs, w2[...])
    masks = [jnp.where(low, 0.0, block(left, 544, RF))] + [edge_a1[k].astype(F32) for k in range(6)]
    masks += [jnp.where(low, block(right, 544, RF), 0.0)]
    for k in range(8):
        grad = jnp.where(masks[k] > 0, out[k * RF : (k + 1) * RF, :], 0.0)
        grad1[:, lanes(k)] = grad.astype(BF16)
    total = part[...] + dot(grad1[:, 0:512], w1[0 : 4 * L, :]) + dot(grad1[:, 512:1024], w1[30 * L : 34 * L, :])
    sums[0, 8:152, :] = total
    sums[0, 0:8, :] = jnp.zeros((8, 256), F32)
    sums[0, 152:160, :] = jnp.zeros((8, 256), F32)
    log = sums[0, 9:153, 0:128] + swap_halves(sums[0, 8:152, 0:128]) + sums[0, 7:151, 128:256]
    pad_f[8:152, :] = log * factor[...]
    for d in range(4):
        out_ref[d] = pad_f[15 + 32 * d : 55 + 32 * d, 0:64]


def synthesis_kernel(place, grads, own, left, right, far, filters, table, window, out_ref, pieces, spec_re, spec_im):
    mel = place[0]
    power = jnp.zeros((40, HOP), F32)
    for j in range(4):
        power = power + dot(grads[j].astype(BF16), filters[64 * j : 64 * (j + 1), :])
    for ref, at, step in ((own, 0, 0), (left, 688, 3), (far, 0, 2), (right, 688, 1)):
        k = lax.rem(mel + step, 4)
        span = pl.ds(pl.multiple_of(k * 128, 128), 128)
        spec_re[:, span] = ref[at : at + 48, :].astype(F32)
        spec_im[:, span] = ref[at + 48 : at + 96, :].astype(F32)
    pieces[:, 0:512] = 2.0 * power * spec_re[0:40, :]
    pieces[:, 512:1024] = 2.0 * power * spec_im[0:40, :]
    odd = lax.broadcasted_iota(jnp.int32, (32, 1024), 1) % 2 == 1
    earlier = pieces[0:32, :]
    earlier = jnp.where(odd, -earlier, earlier)
    both = jnp.concatenate([pieces[1:33, :], earlier], axis=0).astype(BF16)
    frames = dot(both, table[...])
    wave = frames[0:32] * window[0:1, :] + frames[32:64] * window[1:2, :]
    for q in range(4):
        out_ref[pl.ds(q, 32, stride=4), :] = wave[:, q * 128 : (q + 1) * 128]


def dft_constants():
    k = np.arange(512)[:, None]
    n = np.arange(512)[None, :]
    angle = (k * n % NFFT) * (2.0 * np.pi / NFFT)
    table = np.concatenate([np.cos(angle), -np.sin(angle)], axis=0).astype(np.float32)
    points = np.arange(NFFT) * (2.0 * np.pi / NFFT)
    window = (0.5 - 0.5 * np.cos(points)) * NFFT ** (-0.5)
    rows = np.zeros((8, HOP), np.float32)
    rows[0:2] = window.reshape(2, HOP)
    return jnp.asarray(table).astype(BF16), jnp.asarray(rows)


def shards(
    a1, a2, a3, a4, t1, t2, kernel_one, kernel_two, kernel_three, kernel_four,
    mel_power, loudness, filters, re, im,
):
    size = lax.axis_size("tm")
    place = lax.axis_index("mel").astype(jnp.int32).reshape(1)
    end, top = pack_rows(a4, a3, a2, a1, t2, t1, mel_power, re, im)
    before = lax.ppermute(end, "tm", [(i, i + 1) for i in range(size - 1)])
    after = lax.ppermute(top, "tm", [(i + 1, i) for i in range(size - 1)])

    k4 = jnp.transpose(kernel_four, (0, 1, 3, 2))
    k3 = jnp.transpose(kernel_three, (0, 1, 3, 2))
    k3 = jnp.concatenate([k3, k3], axis=3)
    k2 = jnp.transpose(kernel_two, (0, 1, 3, 2))
    k2 = jnp.concatenate([k2, k2], axis=3)
    k1 = jnp.transpose(kernel_one.reshape(9, C1)).astype(F32)
    k1 = jnp.concatenate([k1, k1], axis=0)
    w4, w3, w2, w1 = call(
        weights_kernel,
        [((1536, 256), BF16), ((1536, 256), BF16), ((768, L), BF16), ((34 * L, 256), BF16)],
        [],
        (k4, k3, k2, k1),
        limit=8,
    )
    left_out, right_out, far_out, own = call(
        pack_columns_kernel,
        [((ROWS_M, L), BF16), ((ROWS_M, L), BF16), ((96, L), BF16), ((96, L), BF16)],
        [
            ((2, 16, 4096), F32),
            ((8, 8, 4096), F32),
            ((2, 8, 2048), F32),
            ((2, 8, 2048), F32),
            ((160, 256), F32),
            ((4, 96, L), BF16),
        ],
        (place, a4, a3, a2, a1, t2, t1, re, im, before, after),
        specs=[SMEM] + [VMEM] * 10,
        limit=12,
    )
    ring = [(i, (i + 1) % 4) for i in range(4)]
    back = [(j, i) for i, j in ring]
    from_left = lax.ppermute(right_out, "mel", ring)
    from_right = lax.ppermute(left_out, "mel", back)
    far = lax.ppermute(far_out, "mel", [(i, (i + 2) % 4) for i in range(4)])
    edges = call(
        interior_kernel,
        [
            ((4, RC, L), BF16),
            ((4, RC, L), BF16),
            ((4, RF, L), BF16),
            ((2, RC, L), BF16),
            ((4, RF, L), BF16),
            ((4, RC, L), F32),
            ((6, RF, L), BF16),
            ((RF, 256), F32),
            ((RF, L), F32),
        ],
        [
            ((2, 16, 4096), F32),
            ((8, 8, 4096), F32),
            ((2, 8, 2048), F32),
            ((2, 8, 2048), F32),
            ((3, 16, RC, L), BF16),
            ((3, 16, RC, L), BF16),
            ((3, 15, RC, L), BF16),
            ((3, 15, RC, L), BF16),
            ((3, 27, RF, L), BF16),
            ((RF, 26 * L), BF16),
            ((96, L), F32),
            ((160, L), F32),
            ((RC, 2048), F32),
        ],
        (a4, a3, a2, a1, t2, t1, before, after, mel_power, loudness.reshape(1, 64), w4, w3, w2, w1),
        limit=36,
        flops=1500000000,
    )
    (grads,) = call(
        edge_kernel,
        [((4, 40, 64), F32)],
        [
            ((3, 12, RC, L), BF16),
            ((3, 12, RC, L), BF16),
            ((3, 10, RF, L), BF16),
            ((RF, 8 * L), BF16),
            ((96, L), F32),
            ((160, L), F32),
            ((1, 160, 256), F32),
        ],
        (from_left, from_right, *edges, w4, w3, w2, w1),
        limit=16,
    )
    grads = lax.all_to_all(grads, "mel", 0, 0, tiled=True)
    table, window = dft_constants()
    turned = jnp.transpose(filters).astype(BF16)
    (wave,) = call(
        synthesis_kernel,
        [((128, 128), F32)],
        [((40, 1024), F32), ((48, 512), F32), ((48, 512), F32)],
        (place, grads, own, from_left, from_right, far, turned, table, window),
        specs=[SMEM] + [VMEM] * 8,
        limit=8,
    )
    return wave.reshape(-1)


def solution(mesh):
    return jax.shard_map(
        shards,
        mesh=mesh,
        in_specs=(
            P("tm", "mel"),
            P("tm", "mel"),
            P("tm", "mel"),
            P("tm", "mel"),
            P("tm", "mel"),
            P("tm", "mel"),
            P(),
            P(),
            P(),
            P(),
            P("tm", "mel"),
            P("mel"),
            P(),
            P("tm", "mel"),
            P("tm", "mel"),
        ),
        out_specs=P(("tm", "mel")),
        check_vma=False,
    )
```

```python
import numpy as np
import jax
import jax.numpy as jnp
from jax import lax
from jax.experimental import pallas as pl
from jax.experimental.pallas import tpu as pltpu
from jax.sharding import PartitionSpec as P

F32 = jnp.float32
BF16 = jnp.bfloat16
C1 = 64
C2 = 128
NFFT = 1024
HOP = 512
L = 128
RC = 80
RF = 144
VMEM = pl.BlockSpec(memory_space=pltpu.VMEM)
SMEM = pl.BlockSpec(memory_space=pltpu.SMEM)
ROWS_M = 784


def lanes(index, width=L):
    return pl.ds(index * width, width)


def dot(lhs, rhs):
    return jnp.dot(lhs, rhs, preferred_element_type=F32)


def dot_rows(lhs, rhs):
    return lax.dot_general(lhs, rhs, (((1,), (1,)), ((), ())), preferred_element_type=F32)


def swap_halves(value):
    return pltpu.roll(value, 64, axis=1)


def lower_lanes(shape):
    return lax.broadcasted_iota(jnp.int32, shape, 1) < 64


def pinned(*values):
    return [pltpu.with_memory_space_constraint(value, pltpu.HBM) for value in values]


def call(kernel, outs, scratch, args, specs=None, limit=24, flops=0, moved=1 << 20):
    return pl.pallas_call(
        kernel,
        out_shape=[jax.ShapeDtypeStruct(s, d) for s, d in outs],
        in_specs=specs or [VMEM] * len(args),
        out_specs=[VMEM] * len(outs),
        scratch_shapes=[pltpu.VMEM(s, d) for s, d in scratch],
        compiler_params=pltpu.CompilerParams(vmem_limit_bytes=limit << 20),
        cost_estimate=pl.CostEstimate(flops=flops, bytes_accessed=moved, transcendentals=0),
    )(*args)


def fetch(copies, sems):
    started = [pltpu.make_async_copy(s, d, sems.at[k]) for k, (s, d) in enumerate(copies)]
    for copy in started:
        copy.start()
    return started


def pack_rows_kernel(
    a4, a3, a2, a1, t2, t1, re, im, mel, end_out, top_out, wide, half, mel_end, spec_end, tmp, end, top, sems
):
    copies = []
    for k, (ref, rows) in enumerate(((a4, 64), (a3, 64), (a2, 128), (a1, 128))):
        copies += [(ref.at[rows - 16 : rows, :], wide.at[2 * k]), (ref.at[0:16, :], wide.at[2 * k + 1])]
    for k, (ref, rows) in enumerate(((t2, 32), (t1, 64))):
        copies += [(ref.at[rows - 16 : rows, :], half.at[2 * k]), (ref.at[0:16, :], half.at[2 * k + 1])]
    copies += [(mel, mel_end), (re.at[120:128, :], spec_end.at[0]), (im.at[120:128, :], spec_end.at[1])]
    started = fetch(copies, sems)
    end[...] = jnp.zeros_like(end)
    top[...] = jnp.zeros_like(top)
    for k, (dest, first, count, row) in enumerate(
        (
            (end, 12, 4, 0),
            (top, 0, 4, 0),
            (end, 13, 3, 4),
            (top, 0, 2, 4),
            (end, 12, 4, 7),
            (top, 0, 2, 6),
            (end, 14, 2, 11),
            (top, 0, 1, 8),
        )
    ):
        started[k].wait()
        tmp[...] = wide[k].astype(F32)
        dest[row : row + count, :] = tmp[first : first + count, :]
    for k, (dest, first, count, row) in enumerate(((end, 14, 2, 13), (top, 0, 2, 9), (end, 14, 2, 14), (top, 0, 1, 10))):
        started[8 + k].wait()
        tmp[:, 0:2048] = half[k].astype(F32)
        for n in range(count):
            dest[row : row + 1, n * 2048 : (n + 1) * 2048] = tmp[first + n : first + n + 1, 0:2048]
    for copy in started[12:]:
        copy.wait()
    value = jnp.transpose(mel_end[...])[127:128, :]
    head = value.astype(BF16).astype(F32)
    end[15:16, 0:64] = head
    end[15:16, 128:192] = value - head
    end[15:16, 256:384] = spec_end[0, 7:8, :]
    end[15:16, 384:512] = spec_end[1, 7:8, :]
    end_out[...] = end[...].astype(BF16)
    top_out[...] = top[...].astype(BF16)


def pack_rows(*args):
    return pl.pallas_call(
        pack_rows_kernel,
        out_shape=[jax.ShapeDtypeStruct((16, 4096), BF16)] * 2,
        in_specs=[pl.BlockSpec(memory_space=pltpu.HBM)] * 9,
        out_specs=[VMEM] * 2,
        scratch_shapes=[
            pltpu.VMEM((8, 16, 4096), BF16),
            pltpu.VMEM((4, 16, 2048), BF16),
            pltpu.VMEM((64, 128), F32),
            pltpu.VMEM((2, 8, 128), F32),
            pltpu.VMEM((16, 4096), F32),
            pltpu.VMEM((16, 4096), F32),
            pltpu.VMEM((16, 4096), F32),
            pltpu.SemaphoreType.DMA((15,)),
        ],
        compiler_params=pltpu.CompilerParams(vmem_limit_bytes=8 << 20),
        cost_estimate=pl.CostEstimate(flops=0, bytes_accessed=4 << 20, transcendentals=0),
    )(*args)


def halo_tiles(before, after, raw, tiles, tiles_two, tiles_one, span):
    raw[0, :, span] = before[:, span].astype(F32)
    raw[1, :, span] = after[:, span].astype(F32)
    for k, (dest, first, count, side) in enumerate(
        (
            (4, 0, 4, 0),
            (5, 4, 3, 0),
            (4, 7, 4, 0),
            (6, 11, 2, 0),
            (0, 0, 4, 1),
            (0, 4, 2, 1),
            (0, 6, 2, 1),
            (0, 8, 1, 1),
        )
    ):
        tiles[k, :, span] = jnp.zeros_like(tiles[k, :, span])
        tiles[k, dest : dest + count, span] = raw[side, first : first + count, span]


def target_tiles(before, after, raw, tiles_two, tiles_one):
    raw[0] = before[...].astype(F32)
    raw[1] = after[...].astype(F32)
    tiles_two[...] = jnp.zeros_like(tiles_two)
    tiles_one[...] = jnp.zeros_like(tiles_one)
    for k in range(2):
        half = slice(k * 2048, (k + 1) * 2048)
        tiles_two[0, 6 + k : 7 + k, :] = raw[0, 13:14, half]
        tiles_two[1, k : k + 1, :] = raw[1, 9:10, half]
        tiles_one[0, 6 + k : 7 + k, :] = raw[0, 14:15, half]
    tiles_one[1, 0:1, :] = raw[1, 10:11, 0:2048]


def padded(ref, tiles, kind, span):
    return jnp.concatenate(
        [tiles[kind, :, span], ref[:, span].astype(F32), tiles[kind + 4, :, span]], axis=0
    )


def padded_edge(own, tiles, kind, span):
    return jnp.concatenate([tiles[kind, :, span], own.astype(F32), tiles[kind + 4, :, span]], axis=0)


def repeat_rows_matrix():
    r = lax.broadcasted_iota(jnp.int32, (RC, 48), 0)
    x = lax.broadcasted_iota(jnp.int32, (RC, 48), 1)
    return jnp.where(x == lax.shift_right_logical(r, 1) + 4, 1.0, 0.0).astype(BF16)


def repeated_target(own, tiles, span):
    values = jnp.concatenate([tiles[0, :, span], own.astype(F32), tiles[1, :, span]], axis=0)
    return dot(repeat_rows_matrix(), values.astype(BF16))


def pooled_grads(first, second, target):
    both = jnp.maximum(first, 0.0) + jnp.maximum(second, 0.0)
    cells = both.reshape(RC // 8, 8, L)
    even = lax.broadcasted_iota(jnp.int32, cells.shape, 1) % 2 == 0
    other = jnp.where(even, pltpu.roll(cells, 7, axis=1), pltpu.roll(cells, 1, axis=1))
    feat = 0.25 * (cells + other).reshape(RC, L)
    diff = 0.25 * (feat - target)
    return jnp.where(first > 0, diff, 0.0), jnp.where(second > 0, diff, 0.0)


def lane_doubled(value, upper):
    swapped = swap_halves(value)
    low = lower_lanes(value.shape)
    return jnp.where(low, swapped, value) if upper else jnp.where(low, value, swapped)


def pack_columns_kernel(
    place, e4, e3, e2, e1, u2, u1, own_spec, before, after,
    left_out, right_out, far_out, own_out, raw, tiles, tiles_two, tiles_one, spec, blocks,
):
    target_tiles(before, after, raw, tiles_two, tiles_one)
    for span in (slice(0, 512), slice(3584, 4096)):
        halo_tiles(before, after, raw, tiles, tiles_two, tiles_one, span)
    mel = place[0]
    spec[...] = jnp.zeros_like(spec)
    spec[8:136, 0:128] = own_spec[0]
    spec[8:136, 128:256] = own_spec[1]
    spec[7:8, :] = raw[0, 15:16, 256:512]
    for d in range(4):
        part = spec[7 + 32 * d : 55 + 32 * d, :]
        blocks[d, 0:48, :] = part[:, 0:128].astype(BF16)
        blocks[d, 48:96, :] = part[:, 128:256].astype(BF16)
    own_out[...] = blocks[mel]
    far_out[...] = blocks[lax.rem(mel + 2, 4)]
    left_out[688:784, :] = blocks[lax.rem(mel + 3, 4)]
    right_out[688:784, :] = blocks[lax.rem(mel + 1, 4)]
    keep_left = jnp.where(mel > 0, 1.0, 0.0).astype(F32)
    keep_right = jnp.where(mel < 3, 1.0, 0.0).astype(F32)
    for s, (out, keep, pairs, wanted, three, edge, upper) in enumerate((
        (left_out, keep_left, (0, 1), (0, 1, 2), (0, 1), 0, False),
        (right_out, keep_right, (14, 15), (29, 30, 31), (30, 31), 31, True),
    )):
        for p in pairs:
            columns = [
                padded_edge(e4[s, :, lanes((2 * p + k) % 4)], tiles, 0, lanes(2 * p + k)) for k in range(2)
            ]
            target = repeated_target(u2[s, :, lanes(p % 2)], tiles_two, lanes(p))
            for k, grad in enumerate(pooled_grads(*columns, target)):
                if 2 * p + k in wanted:
                    at = wanted.index(2 * p + k) * RC
                    out[at : at + RC, :] = (grad * keep).astype(BF16)
        for k, c in enumerate(three):
            at = 240 + k * RC
            value = padded_edge(e3[s, :, lanes(c % 4)], tiles, 1, lanes(c))
            out[at : at + RC, :] = (value * keep).astype(BF16)
        out[400:544, :] = (padded_edge(e2[s, :, lanes(edge % 4)], tiles, 2, lanes(edge)) * keep).astype(BF16)
        one = padded_edge(e1[s, :, lanes(edge % 4)], tiles, 3, lanes(edge))
        low_target = jnp.concatenate(
            [
                tiles_one[0, :, lanes(edge // 2)],
                u1[s].astype(F32),
                tiles_one[1, :, lanes(edge // 2)],
            ],
            axis=0,
        )
        low_target = jnp.concatenate([low_target, jnp.zeros((RF - RC, L), F32)], axis=0)
        swapped = swap_halves(low_target)
        low = lower_lanes((RF, L))
        joined = jnp.where(low, swapped, one) if upper else jnp.where(low, one, swapped)
        out[544:688, :] = (joined * keep).astype(BF16)


def prepare_kernel(
    a4, a3, a2, a1, t2, t1, re, im, k4_hbm, k3_hbm, k2_hbm, k1_hbm, filters_hbm, packed,
    w4, w3, w2, w1, e4, e3, e2, e1, u2, u1, spec, bank, k4, k3, k2, k1, filters, sems,
):
    copies = [(k4_hbm, k4), (k3_hbm, k3), (k2_hbm, k2), (k1_hbm, k1), (filters_hbm, filters)]
    for k, first in enumerate((0, 3584)):
        for ref, dest in ((a4, e4), (a3, e3), (a2, e2), (a1, e1)):
            copies.append((ref.at[:, first : first + 512], dest.at[k]))
    for k in range(2):
        copies.append((t2.at[:, k * 1792 : k * 1792 + 256], u2.at[k]))
        copies.append((t1.at[:, k * 1920 : k * 1920 + 128], u1.at[k]))
    copies += [(re, spec.at[0]), (im, spec.at[1])]
    started = fetch(copies, sems)
    for copy in started[0:4]:
        copy.wait()
    empty = jnp.zeros((L, L), BF16)
    low = lower_lanes((64, L))
    for i in range(3):
        for b in range(4):
            span = lanes(i * 4 + b)
            for a in range(2):
                j = 1 + a - b
                fits = -1 <= j <= 1
                w4[a * L : (a + 1) * L, span] = k4[i, j + 1] if fits else empty
                for half in range(2):
                    row = a * L + half * 64
                    w3[row : row + 64, span] = k3[i, j + 1] if fits else empty[0:64]
        for b in range(0, 4, 2):
            for a in range(2):
                parts = []
                for k in range(2):
                    j = 1 + a - b - k
                    if -1 <= j <= 1:
                        parts.append(k2[i, j + 1].astype(F32))
                    else:
                        parts.append(jnp.zeros((64, 64), F32))
                w2[a * 64 : (a + 1) * 64, lanes(i * 2 + b // 2)] = jnp.concatenate(parts, axis=1).astype(BF16)
    w1[...] = jnp.zeros_like(w1)
    row = lax.broadcasted_iota(jnp.int32, (16, L), 0)
    low = lower_lanes((16, L))
    for i in range(3):
        taps = [jnp.concatenate([k1[i, j : j + 1, :].astype(F32)] * 2, axis=1) for j in range(3)]
        taps = [jnp.broadcast_to(tap, (16, L)) for tap in taps]
        zero = jnp.zeros((16, L), F32)
        lines = [
            jnp.where(low, taps[d] if d < 3 else zero, taps[d - 1] if d > 0 else zero) for d in range(4)
        ]
        tiles = {}
        for first in (-3, -1, 1, 3, 5, 7, 9, 11, 13, 15):
            tile = zero
            for d in range(4):
                tile = jnp.where(row == first + d, lines[d], tile)
            tiles[first] = tile.astype(BF16)
        for p in range(-1, 33):
            for t in range(4):
                first = 2 * p - 1 - 16 * t
                if -4 < first < 16:
                    at = i * 64 + t * 16
                    w1[at : at + 16, lanes(p + 1)] = tiles[first]
    started[4].wait()
    bank[...] = filters[...].astype(BF16)
    for copy in started[5:]:
        copy.wait()


def write_shifted(value, rows, pad, stores):
    pad[8 : 8 + rows, :] = value
    for i, store in enumerate(stores):
        store(pad[9 - i : 9 - i + rows, :].astype(BF16))


def pool_rows_matrix():
    r = lax.broadcasted_iota(jnp.int32, (RC, RF), 0)
    x = lax.broadcasted_iota(jnp.int32, (RC, RF), 1)
    return jnp.where(lax.shift_right_logical(x, 1) + 4 == r, 1.0, 0.0).astype(BF16)


def spread_rows_matrix():
    x = lax.broadcasted_iota(jnp.int32, (RF, RC), 0)
    r = lax.broadcasted_iota(jnp.int32, (RF, RC), 1)
    return jnp.where(lax.shift_right_logical(x, 1) + 4 == r, 1.0, 0.0).astype(BF16)


def pooled_low(second):
    rows = dot(pool_rows_matrix(), jnp.maximum(second, 0.0).astype(BF16))
    return 0.25 * (rows + swap_halves(rows))


def joined(parts):
    return jnp.concatenate(parts, axis=-1)


def interior_kernel(
    a4, a3, a2, a1, t2, t1, before, after, mel, loud, w4, w3, w2, w1,
    edge_g4, edge_g3, edge_g2, edge_a3, edge_a2, edge_low, edge_a1, part_out, factor_out,
    raw, tiles, tiles_two, tiles_one, even4, odd4, even3, odd3, back2, grad1, pad_c, pad_f, t2s,
):
    target_tiles(before, after, raw, tiles_two, tiles_one)
    halo_tiles(before, after, raw, tiles, tiles_two, tiles_one, slice(0, 4096))
    pad_c[...] = jnp.zeros_like(pad_c)
    pad_f[...] = jnp.zeros_like(pad_f)
    pad_f[8:136, 0:64] = jnp.transpose(mel[...])
    pad_f[7:8, 0:64] = raw[0, 15:16, 0:64] + raw[0, 15:16, 128:192]
    gain = loud[0:1, :]
    factor_out[...] = jnp.zeros_like(factor_out)
    factor_out[:, 0:64] = gain / (1.0 + gain * pad_f[0:RF, 0:64])
    t2s[...] = repeated_target(t2[...], tiles_two, slice(0, 2048))

    for p in range(16):
        columns = [padded(a4, tiles, 0, lanes(2 * p + k)) for k in range(2)]
        grads = pooled_grads(*columns, t2s[:, lanes(p)])
        if p in (0, 15):
            for k in range(2):
                edge_g4[(0 if p == 0 else 2) + k] = grads[k].astype(BF16)
        for k, store in enumerate((even4, odd4)):
            write_shifted(grads[k], RC, pad_c, [lambda v, i=i: store.__setitem__((i, p), v) for i in range(3)])
    lhs = joined([x for i in range(3) for x in (even4[i, 0:15], odd4[i, 0:15], even4[i, 1:16], odd4[i, 1:16])])
    out = dot_rows(lhs.reshape(15 * RC, 1536), w4[...]).reshape(15, RC, 256)
    for q in range(15):
        for k, store in enumerate((odd3, even3)):
            c = 2 * q + 1 + k
            grad = jnp.where(padded(a3, tiles, 1, lanes(c)) > 0, out[q, :, k * L : (k + 1) * L], 0.0)
            if c in (1, 2, 29, 30):
                edge_g3[(1, 2, 29, 30).index(c)] = grad.astype(BF16)
            write_shifted(grad, RC, pad_c, [lambda v, i=i: store.__setitem__((i, q), v) for i in range(3)])
    for k, c in enumerate((0, 31)):
        edge_a3[k] = padded(a3, tiles, 1, lanes(c)).astype(BF16)
    lhs = joined([x for i in range(3) for x in (odd3[i, 0:14], even3[i, 0:14], odd3[i, 1:15], even3[i, 1:15])])
    out = dot_rows(lhs.reshape(14 * RC, 1536), w3[...]).reshape(14, RC, 256)

    def low_loss(c, second):
        span = lanes(c // 2)
        target = jnp.concatenate([tiles_one[0, :, span], t1[:, span].astype(F32), tiles_one[1, :, span]], axis=0)
        return pooled_low(second) - lane_doubled(target, c % 2 == 1)

    for k, c in enumerate((0, 1, 30, 31)):
        second = padded(a2, tiles, 2, lanes(c))
        edge_a2[k] = second.astype(BF16)
        edge_low[k] = low_loss(c, second)
    spreading = spread_rows_matrix()
    last = None
    for c in range(2, 30):
        second = padded(a2, tiles, 2, lanes(c))
        grad = out[c // 2 - 1, :, (c % 2) * L : (c % 2 + 1) * L] + low_loss(c, second)
        wide = dot(spreading, (0.25 * grad).astype(BF16))
        fine = jnp.where(second > 0, wide, 0.0)
        if c in (2, 3, 28, 29):
            edge_g2[(2, 3, 28, 29).index(c)] = fine.astype(BF16)
        turned = swap_halves(fine)
        if last is not None:
            window = jnp.where(lower_lanes((RF, L)), last, turned)
            write_shifted(window, RF, pad_f, [lambda v, i=i: back2.__setitem__((i, c - 3), v) for i in range(3)])
        last = turned
    lhs = joined([x for i in range(3) for x in (back2[i, 0:26], back2[i, 1:27])])
    out = dot_rows(lhs.reshape(26 * RF, 768), w2[...]).reshape(26, RF, L)
    for p in range(3, 29):
        grad = jnp.where(padded(a1, tiles, 3, lanes(p)) > 0, out[p - 3], 0.0)
        grad1[:, lanes(p - 3)] = grad.astype(BF16)
    for k, p in enumerate((0, 1, 2, 29, 30, 31)):
        edge_a1[k] = padded(a1, tiles, 3, lanes(p)).astype(BF16)
    part_out[...] = dot_rows(grad1[...], w1[:, 4 * L : 30 * L])


def edge_kernel(
    place, far_spec, from_left, from_right, edge_g4, edge_g3, edge_g2, edge_a3, edge_a2, edge_low, edge_a1,
    part, factor, w4, w3, w2, w1, own_out, next_out, far_out, last_out,
    shift4, shift3, back2, grad1, pad_c, pad_f, sums, blocks,
):
    pad_c[...] = jnp.zeros_like(pad_c)
    pad_f[...] = jnp.zeros_like(pad_f)
    zero_c = jnp.zeros((RC, L), F32)
    zero_f = jnp.zeros((RF, L), F32)

    def block(ref, at, rows):
        return ref[at : at + rows, :].astype(F32)

    def put(store, index, value, rows, pad):
        write_shifted(value, rows, pad, [lambda v, i=i: store.__setitem__((i, index), v) for i in range(3)])

    left, right = from_left, from_right
    columns = [zero_c] + [block(left, k * RC, RC) for k in range(3)] + [edge_g4[k].astype(F32) for k in range(4)]
    columns += [block(right, k * RC, RC) for k in range(3)] + [zero_c]
    for k, value in enumerate(columns):
        put(shift4, k, value, RC, pad_c)
    starts = (0, 2, 6, 8)
    lhs = jnp.concatenate(
        [joined([shift4[i, s + b] for i in range(3) for b in range(4)]) for s in starts], axis=0
    )
    out = dot_rows(lhs, w4[...])
    masks = [zero_c, block(left, 240, RC), block(left, 240 + RC, RC), edge_a3[0].astype(F32)]
    masks += [edge_a3[1].astype(F32), block(right, 240, RC), block(right, 240 + RC, RC), zero_c]
    threes = []
    for k in range(8):
        value = out[(k // 2) * RC : (k // 2 + 1) * RC, (k % 2) * L : (k % 2 + 1) * L]
        threes.append(jnp.where(masks[k] > 0, value, 0.0))
    columns = threes[0:4] + [edge_g3[k].astype(F32) for k in range(4)] + threes[4:8]
    for k, value in enumerate(columns):
        put(shift3, k, value, RC, pad_c)
    lhs = jnp.concatenate(
        [joined([shift3[i, s + b] for i in range(3) for b in range(4)]) for s in starts], axis=0
    )
    out = dot_rows(lhs, w3[...])
    spreading = spread_rows_matrix()
    twos = []
    for k in (1, 2, 3, 4, 5, 6):
        grad = out[(k // 2) * RC : (k // 2 + 1) * RC, (k % 2) * L : (k % 2 + 1) * L]
        if k in (1, 6):
            ref = left if k == 1 else right
            second = block(ref, 400, RF)
            target = block(ref, 544, RC)
            low = pooled_low(second) - lane_doubled(target, k == 6)
        else:
            second = edge_a2[k - 2].astype(F32)
            low = edge_low[k - 2]
        wide = dot(spreading, (0.25 * (grad + low)).astype(BF16))
        twos.append(jnp.where(second > 0, wide, 0.0))
    turned = [swap_halves(x) for x in twos]
    inner = [swap_halves(edge_g2[k].astype(F32)) for k in range(4)]
    low = lower_lanes((RF, L))
    chain = [zero_f] + turned[0:3] + inner[0:2]
    windows = [jnp.where(low, chain[k], chain[k + 1]) for k in range(5)]
    chain = inner[2:4] + turned[3:6] + [zero_f]
    windows += [jnp.where(low, chain[k], chain[k + 1]) for k in range(5)]
    for k, value in enumerate(windows):
        put(back2, k, value, RF, pad_f)
    lhs = jnp.concatenate(
        [joined([back2[i, s + b] for i in range(3) for b in range(2)]) for s in (0, 1, 2, 3, 5, 6, 7, 8)], axis=0
    )
    out = dot_rows(lhs, w2[...])
    masks = [jnp.where(low, 0.0, block(left, 544, RF))] + [edge_a1[k].astype(F32) for k in range(6)]
    masks += [jnp.where(low, block(right, 544, RF), 0.0)]
    for k in range(8):
        grad = jnp.where(masks[k] > 0, out[k * RF : (k + 1) * RF, :], 0.0)
        grad1[:, lanes(k)] = grad.astype(BF16)
    total = part[...] + dot_rows(grad1[:, 0:512], w1[:, 0 : 4 * L]) + dot_rows(grad1[:, 512:1024], w1[:, 30 * L : 34 * L])
    sums[...] = jnp.zeros_like(sums)
    sums[8:152, 0:192] = total
    log = sums[9:153, 0:128] + swap_halves(sums[8:152, 0:128]) + sums[7:151, 128:256]
    grad = log * factor[...]
    mel = place[0]
    odd = lax.rem(mel, 2) == 1
    pad_f[8:152, :] = jnp.where(odd, swap_halves(grad), grad)
    for d in range(4):
        blocks[d] = pad_f[15 + 32 * d : 63 + 32 * d, :].astype(BF16) if d < 3 else jnp.concatenate(
            [pad_f[111:151, :], jnp.zeros((8, L), F32)], axis=0
        ).astype(BF16)
    own_out[...] = blocks[mel]
    next_out[...] = blocks[lax.rem(mel + 1, 4)]
    last_out[...] = blocks[lax.rem(mel + 3, 4)]
    far_out[0:48, :] = blocks[lax.rem(mel + 2, 4)]
    far_out[48:144, :] = far_spec[...]


def synthesis_kernel(
    place, grad0, grad1, grad2, grad3, own, left, right, bank, table, window, out_ref, pieces, spec_re, spec_im, mels
):
    mel = place[0]
    mels[...] = jnp.zeros_like(mels)
    sources = ((grad0, own, 0, 0), (grad1, left, 688, 3), (grad2, grad2, 48, 2), (grad3, right, 688, 1))
    for grad, ref, at, step in sources:
        k = lax.rem(mel + step, 4)
        half = pl.ds(pl.multiple_of(lax.div(k, 2) * 128, 128), 128)
        mels[:, half] = mels[:, half] + grad[0:48, :].astype(F32)
        span = pl.ds(pl.multiple_of(k * 128, 128), 128)
        spec_re[:, span] = ref[at : at + 48, :].astype(F32)
        spec_im[:, span] = ref[at + 48 : at + 96, :].astype(F32)
    power = dot_rows(mels[...].astype(BF16), bank[...])[0:40]
    pieces[:, 0:512] = 2.0 * power * spec_re[0:40, :]
    pieces[:, 512:1024] = 2.0 * power * spec_im[0:40, :]
    odd = lax.broadcasted_iota(jnp.int32, (32, 1024), 1) % 2 == 1
    earlier = pieces[0:32, :]
    earlier = jnp.where(odd, -earlier, earlier)
    both = jnp.concatenate([pieces[1:33, :], earlier], axis=0).astype(BF16)
    frames = dot(both, table[...])
    wave = frames[0:32] * window[0:1, :] + frames[32:64] * window[1:2, :]
    for q in range(4):
        out_ref[pl.ds(q, 32, stride=4), :] = wave[:, q * 128 : (q + 1) * 128]


def dft_constants():
    k = np.arange(512)[:, None]
    n = np.arange(512)[None, :]
    angle = (k * n % NFFT) * (2.0 * np.pi / NFFT)
    table = np.concatenate([np.cos(angle), -np.sin(angle)], axis=0).astype(np.float32)
    points = np.arange(NFFT) * (2.0 * np.pi / NFFT)
    window = (0.5 - 0.5 * np.cos(points)) * NFFT ** (-0.5)
    rows = np.zeros((8, HOP), np.float32)
    rows[0:2] = window.reshape(2, HOP)
    return jnp.asarray(table).astype(BF16), jnp.asarray(rows)


def shards(
    a1, a2, a3, a4, t1, t2, kernel_one, kernel_two, kernel_three, kernel_four,
    mel_power, loudness, filters, re, im,
):
    size = lax.axis_size("tm")
    place = lax.axis_index("mel").astype(jnp.int32).reshape(1)
    mel_rows = jnp.transpose(mel_power)
    inputs = pinned(a4, a3, a2, a1, t2, t1, re, im)
    end, top = pack_rows(*inputs, *pinned(mel_rows))
    before = lax.ppermute(end, "tm", [(i, i + 1) for i in range(size - 1)])
    after = lax.ppermute(top, "tm", [(i + 1, i) for i in range(size - 1)])

    hbm = pl.BlockSpec(memory_space=pltpu.HBM)
    prepared = pl.pallas_call(
        prepare_kernel,
        out_shape=[
            jax.ShapeDtypeStruct(shape, kind)
            for shape, kind in (
                ((256, 1536), BF16),
                ((256, 1536), BF16),
                ((128, 768), BF16),
                ((192, 34 * L), BF16),
                ((2, 64, 512), BF16),
                ((2, 64, 512), BF16),
                ((2, 128, 512), BF16),
                ((2, 128, 512), BF16),
                ((2, 32, 256), BF16),
                ((2, 64, 128), BF16),
                ((2, 128, 128), F32),
                ((512, 256), BF16),
            )
        ],
        in_specs=[hbm] * 13 + [VMEM],
        out_specs=[VMEM] * 12,
        scratch_shapes=[
            pltpu.VMEM((3, 3, 128, 128), BF16),
            pltpu.VMEM((3, 3, 64, 128), BF16),
            pltpu.VMEM((3, 3, 64, 64), BF16),
            pltpu.VMEM((3, 3, 64), BF16),
            pltpu.VMEM((512, 256), F32),
            pltpu.SemaphoreType.DMA((19,)),
        ],
        compiler_params=pltpu.CompilerParams(vmem_limit_bytes=10 << 20),
        cost_estimate=pl.CostEstimate(flops=0, bytes_accessed=8 << 20, transcendentals=0),
    )(
        *inputs,
        *pinned(kernel_four, kernel_three, kernel_two, kernel_one.reshape(3, 3, C1), filters),
        end,
    )
    w4, w3, w2, w1, e4, e3, e2, e1, u2, u1, spec, bank = prepared
    left_out, right_out, far_spec, own = call(
        pack_columns_kernel,
        [((ROWS_M, L), BF16), ((ROWS_M, L), BF16), ((96, L), BF16), ((96, L), BF16)],
        [
            ((2, 16, 4096), F32),
            ((8, 8, 4096), F32),
            ((2, 8, 2048), F32),
            ((2, 8, 2048), F32),
            ((160, 256), F32),
            ((4, 96, L), BF16),
        ],
        (place, e4, e3, e2, e1, u2, u1, spec, before, after),
        specs=[SMEM] + [VMEM] * 9,
        limit=8,
    )
    ring = [(i, (i + 1) % 4) for i in range(4)]
    back = [(j, i) for i, j in ring]
    from_left = lax.ppermute(right_out, "mel", ring)
    from_right = lax.ppermute(left_out, "mel", back)
    edges = call(
        interior_kernel,
        [
            ((4, RC, L), BF16),
            ((4, RC, L), BF16),
            ((4, RF, L), BF16),
            ((2, RC, L), BF16),
            ((4, RF, L), BF16),
            ((4, RC, L), F32),
            ((6, RF, L), BF16),
            ((RF, 192), F32),
            ((RF, L), F32),
        ],
        [
            ((2, 16, 4096), F32),
            ((8, 8, 4096), F32),
            ((2, 8, 2048), F32),
            ((2, 8, 2048), F32),
            ((3, 16, RC, L), BF16),
            ((3, 16, RC, L), BF16),
            ((3, 15, RC, L), BF16),
            ((3, 15, RC, L), BF16),
            ((3, 27, RF, L), BF16),
            ((RF, 26 * L), BF16),
            ((96, L), F32),
            ((160, L), F32),
            ((RC, 2048), F32),
        ],
        (a4, a3, a2, a1, t2, t1, before, after, mel_rows, loudness.reshape(1, 64), w4, w3, w2, w1),
        limit=36,
        flops=1500000000,
    )
    grad0, out1, out2, out3 = call(
        edge_kernel,
        [((48, L), BF16), ((48, L), BF16), ((144, L), BF16), ((48, L), BF16)],
        [
            ((3, 12, RC, L), BF16),
            ((3, 12, RC, L), BF16),
            ((3, 10, RF, L), BF16),
            ((RF, 8 * L), BF16),
            ((96, L), F32),
            ((160, L), F32),
            ((160, 256), F32),
            ((4, 48, L), BF16),
        ],
        (place, far_spec, from_left, from_right, *edges, w4, w3, w2, w1),
        specs=[SMEM] + [VMEM] * 16,
        limit=12,
    )
    grad2 = lax.ppermute(out2, "mel", [(i, (i + 2) % 4) for i in range(4)])
    grad1 = lax.ppermute(out1, "mel", ring)
    grad3 = lax.ppermute(out3, "mel", back)
    table, window = dft_constants()
    (wave,) = call(
        synthesis_kernel,
        [((128, 128), F32)],
        [((40, 1024), F32), ((48, 512), F32), ((48, 512), F32), ((48, 256), F32)],
        (place, grad0, grad1, grad2, grad3, own, from_left, from_right, bank, table, window),
        specs=[SMEM] + [VMEM] * 10,
        limit=8,
    )
    return wave.reshape(-1)


def solution(mesh):
    return jax.shard_map(
        shards,
        mesh=mesh,
        in_specs=(
            P("tm", "mel"),
            P("tm", "mel"),
            P("tm", "mel"),
            P("tm", "mel"),
            P("tm", "mel"),
            P("tm", "mel"),
            P(),
            P(),
            P(),
            P(),
            P("tm", "mel"),
            P("mel"),
            P(),
            P("tm", "mel"),
            P("tm", "mel"),
        ),
        out_specs=P(("tm", "mel")),
        check_vma=False,
    )
```
